512 devices in a mesh: width: 16 (over z), cb: 16 (over x, y), row: 2 (over core).
Axes of the slice: x: 4, y: 4, z: 16, core: 2. Of those that a mesh axis runs over, the one named last changes fastest.
Arguments:
- weights: bfloat16 [14336, 8192], P(('cb', 'row'), 'width'), as said below
- dir_codes: int32 [14336, 1024], P(('cb', 'row'), 'width'), may hold values from 0 to 65535
- norm_bins: int32 [14336, 1024], P(('cb', 'row'), 'width'), may hold values from 0 to 255, as said below
Outputs:
- codewords: float32 [4096, 128], P('cb')
- norm_levels: float32 [256], replicated
The draws below stay inside these ranges and needn't reach their ends.
Inputs may be any that keep to these rules, and one draw needn't show every extreme that they name: `weights`: real-valued entries, rows of differing scales. `norm_bins`: the bins of one row all lie in one aligned run of 16 consecutive bins.
All inputs are finite; a program needn't handle non-finite values.
Results may differ from the reference program's by a relative error of at most 0.0003.
Values sent between devices are 32-bit elements; how exact they have to be, the bound alone decides.
No kernel may reach another device: no remote copies, remote signals or barrier semaphores. Data moves between devices by JAX's collectives and lax.ppermute only.
A program may use at most 128 MiB of HBM per device.

```python
import math
import jax
import jax.numpy as jnp
import numpy as np
from jax import lax

WIDTH = 8192
CODES = 65536
NBINS = 256
ROWS = 14336
GROUPS = 1024


def row_levels(key):
    base_levels = jnp.arange(ROWS, dtype=jnp.int32) % 16
    return jax.random.permutation(jax.random.fold_in(key, 11), base_levels)


def draw_weights(key, part):
    levels = row_levels(key)
    position = jnp.arange(ROWS, dtype=jnp.float32) / ROWS
    entries = jnp.clip(jax.random.normal(jax.random.fold_in(key, 12), (ROWS, WIDTH), jnp.float32), -6.0, 6.0)
    row_ramp = 1.0 + 2.0 * position
    scales = jnp.power(jnp.float32(1.25), levels.astype(jnp.float32)) * row_ramp
    return (entries * scales[:, None]).astype(jnp.bfloat16)


def draw_norm_bins(key, part):
    levels = row_levels(key)
    run_width = NBINS // 16
    offsets = jax.random.randint(jax.random.fold_in(key, 14), (ROWS, GROUPS), 0, run_width, dtype=jnp.int32)
    return levels[:, None] * run_width + offsets


def touch_ends(drawn, own_key, least, top_value):
    place = [jax.random.randint(jax.random.fold_in(own_key, axis), (), 0, length) for axis, length in enumerate(drawn.shape)]
    widest = drawn.shape.index(max(drawn.shape))
    next_to = place[:widest] + [(place[widest] + 1) % drawn.shape[widest]] + place[widest + 1:]
    return drawn.at[tuple(place)].set(least).at[tuple(next_to)].set(top_value)


def rank_bounds(count, slope):
    portions = [(1 << 20) // math.isqrt(grade ** slope) + 1 for grade in range(1, count + 1)]
    deviation = 1 + sum(portions) // (1 << 30)
    return np.cumsum(np.array([max(1, weight // deviation) for weight in portions]))


def ranked(own_key, extent, number_of, skew):
    listing = rank_bounds(number_of, skew)
    pick = jax.random.randint(jax.random.fold_in(own_key, 1), extent, 0, int(listing[number_of - 1]))
    standing = jnp.searchsorted(jnp.asarray(listing, jnp.int32), pick, side="right")
    return jax.random.permutation(jax.random.fold_in(own_key, 2), number_of)[standing].astype(jnp.int32)


def setup_inputs(seed: int = 0) -> dict:
    splits = jax.random.split(jax.random.key(seed), 4)
    return {
        "weights": draw_weights(jax.random.fold_in(splits[3], 71), 0),
        "dir_codes": touch_ends(ranked(splits[1], (ROWS, GROUPS), CODES, 3), jax.random.fold_in(splits[1], 3), 0, CODES - 1).astype(jnp.int32),
        "norm_bins": draw_norm_bins(jax.random.fold_in(splits[3], 71), 0),
    }


def hadamard_rows(row_data):
    row_count, width_now = row_data.shape
    half_span = 1
    while half_span < width_now:
        paired = row_data.reshape(row_count, width_now // (2 * half_span), 2, half_span)
        first = paired[:, :, 0]
        second = paired[:, :, 1]
        row_data = jnp.stack([first + second, first - second], axis=2).reshape(row_count, width_now)
        half_span = half_span * 2
    return row_data

def reference(weights, dir_codes, norm_bins):
    rotated = hadamard_rows(weights.astype(jnp.float32)) * (1.0 / math.sqrt(WIDTH))
    grouped = rotated.reshape(-1, 8)
    group_norms = jnp.sqrt(lax.optimization_barrier(jnp.sum(grouped * grouped, axis=-1)))
    floored = jnp.maximum(group_norms, 1.0)
    directions = grouped / floored[:, None]
    code_sums = jax.ops.segment_sum(directions, dir_codes.reshape(-1), num_segments=CODES)
    lengths = jnp.sqrt(lax.optimization_barrier(jnp.sum(code_sums * code_sums, axis=-1)))
    codewords = (code_sums / jnp.maximum(lengths, 1.0)[:, None]).reshape(CODES // 16, 128)
    log_norms = jnp.log(floored)
    bin_ids = norm_bins.reshape(-1)
    bin_sums = jax.ops.segment_sum(log_norms, bin_ids, num_segments=NBINS)
    bin_counts = jax.ops.segment_sum(jnp.ones_like(log_norms), bin_ids, num_segments=NBINS)
    norm_levels = bin_sums / jnp.maximum(bin_counts, 1.0)
    return (codewords, norm_levels)
```

```python
import math

import jax
import jax.numpy as jnp
from jax import lax
from jax.experimental import pallas as pl
from jax.experimental.pallas import tpu as pltpu
from jax.sharding import PartitionSpec as P

WIDTH = 8192
CODES = 65536
NBINS = 256
SCALING = 1.0 / math.sqrt(WIDTH)
F32 = jnp.float32
I32 = jnp.int32

SOURCES = 16
TILES = 14
CHUNKS = 1
ACCS = 8
CODE_ROWS = CODES // 16


def iota(shape, axis):
    return lax.broadcasted_iota(I32, shape, axis)


def lanes_at(values, index):
    return jnp.take_along_axis(values, index, axis=1, mode="promise_in_bounds")


def vmem(count):
    return [pl.BlockSpec(memory_space=pltpu.VMEM)] * count


def pack_kernel(weights_ref, codes_ref, bins_ref, parts_ref, ints_ref):
    common = jnp.bitwise_and(iota((128, 128), 0), iota((128, 128), 1))
    for shift in (4, 2, 1):
        common = jnp.bitwise_xor(common, common >> shift)
    hadamard = (1 - 2 * jnp.bitwise_and(common, 1)).astype(F32).astype(jnp.bfloat16)
    blocks = [
        jnp.dot(weights_ref[:, 128 * b : 128 * b + 128], hadamard, preferred_element_type=F32)
        for b in range(4)
    ]
    sums = [blocks[0] + blocks[1], blocks[0] - blocks[1], blocks[2] + blocks[3], blocks[2] - blocks[3]]
    blocks = [sums[0] + sums[2], sums[1] + sums[3], sums[0] - sums[2], sums[1] - sums[3]]
    for b in range(4):
        parts_ref[:, b] = blocks[b].reshape(56, 8, 128)
    lane = iota((8, 128), 1)
    own = jnp.bitwise_and(lane, 7) == iota((8, 128), 0)

    def spread(ref, tile):
        padded = jnp.concatenate([ref[pl.ds(pl.multiple_of(tile * 8, 8), 8), :]] * 2, axis=1)
        rows = []
        for b in range(4):
            taken = lanes_at(padded, 16 * b + (lane >> 3))
            rows.append(jnp.sum(jnp.where(own, taken, 0), axis=0, keepdims=True))
        return rows

    def step(tile, carry):
        ints_ref[tile] = jnp.concatenate(spread(codes_ref, tile) + spread(bins_ref, tile), axis=0)
        return carry

    lax.fori_loop(0, 56, step, 0)


def pack(weights, codes, bins):
    return pl.pallas_call(
        pack_kernel,
        out_shape=[
            jax.ShapeDtypeStruct((56, 4, 8, 128), F32),
            jax.ShapeDtypeStruct((56, 8, 128), I32),
        ],
        in_specs=vmem(3),
        out_specs=vmem(2),
        name="pack",
    )(weights, codes, bins)


def sums_kernel(tiles, first, *refs):
    side_ref, at_ref, parts_ref, codes_ref, bins_ref = refs[:5]
    before = refs[5:8] if not first else None
    keep_ref, send_ref, totals_ref = refs[-4 - 2 * 1 - ACCS : -3 - ACCS]
    items, directions_ref = refs[-3 - ACCS : -1 - ACCS], refs[-1 - ACCS]
    accs = refs[-ACCS:]
    lane = iota((8, 128), 1)
    place = iota((8, 128), 0)
    inner = jnp.bitwise_and(lane, 7)
    outer = lane >> 3
    for acc in accs:
        acc[...] = jnp.zeros_like(acc)
    group = (iota((128, 128), 0) >> 3 == iota((128, 128), 1) >> 3).astype(F32)

    def rotate(t, carry):
        z = [parts_ref[h, t] for h in range(SOURCES)]
        for bit in range(4):
            d = 1 << bit
            z = [z[h ^ d] - z[h] if h & d else z[h] + z[h ^ d] for h in range(SOURCES)]
        rotated = jnp.concatenate(z, axis=0) * SCALING
        squares = jnp.dot(
            rotated * rotated, group, precision=lax.Precision.HIGHEST, preferred_element_type=F32
        )
        floored = jnp.maximum(jnp.sqrt(squares), 1.0)
        directions = rotated / floored
        logs = jnp.log(floored)
        packed = []
        for half in range(2):
            log_sum = jnp.zeros((8, 128), F32)
            bin_sum = jnp.zeros((8, 128), I32)
            for j in range(8):
                h = 8 * half + j
                bins = jnp.broadcast_to(bins_ref[h, pl.ds(t, 1), :], (8, 128))
                bins = lanes_at(bins, 8 * outer + place)
                log_sum = log_sum + jnp.where(inner == j, logs[8 * h : 8 * h + 8], 0.0)
                bin_sum = bin_sum + jnp.where(inner == j, bins, 0)
            packed.append((log_sum, bin_sum))
        for h in range(SOURCES):
            directions_ref[h * tiles + t] = directions[8 * h : 8 * h + 8]
        base = packed[0][1] >> 4
        low, high, low_count, high_count = carry
        for offset in range(16):
            log_total = jnp.zeros((8, 128), F32)
            count = jnp.zeros((8, 128), F32)
            for log_sum, bin_sum in packed:
                chosen = jnp.bitwise_and(bin_sum, 15) == offset
                log_total = log_total + jnp.where(chosen, log_sum, 0.0)
                count = count + jnp.where(chosen, 1.0, 0.0)
            log_total = jnp.sum(log_total, axis=1, keepdims=True)
            count = jnp.sum(count, axis=1, keepdims=True)
            target = 16 * base + offset
            at_low, at_high = target == lane, target == lane + 128
            low = low + jnp.where(at_low, log_total, 0.0)
            high = high + jnp.where(at_high, log_total, 0.0)
            low_count = low_count + jnp.where(at_low, count, 0.0)
            high_count = high_count + jnp.where(at_high, count, 0.0)
        return low, high, low_count, high_count

    empty = jnp.zeros((8, 128), F32)
    bin_parts = lax.fori_loop(0, tiles, rotate, (empty,) * 4)
    rows = [jnp.sum(part, axis=0, keepdims=True) for part in bin_parts]
    totals = jnp.concatenate(rows + [jnp.zeros((4, 128), F32)], axis=0)

    def lay_out(n, items_ref):
        h, t = n // tiles, n % tiles
        direction = directions_ref[n]
        codes = jnp.broadcast_to(codes_ref[h, pl.ds(t, 1), :], (8, 128))
        codes = jnp.bitwise_and(codes, 15)
        for k in range(16):
            values = lanes_at(direction, 8 * k + inner)
            slot = lanes_at(codes, 8 * k + place)
            items_ref[8 * k : 8 * k + 8, :] = jnp.where(slot == outer, values, 0.0)

    def add(n, items_ref):
        for k in range(16):
            at = [at_ref[n * 128 + 8 * k + s] for s in range(ACCS)]
            old = [accs[s][pl.ds(at[s], 1), :] for s in range(ACCS)]
            for s in range(ACCS):
                accs[s][pl.ds(at[s], 1), :] = old[s] + items_ref[8 * k + s : 8 * k + s + 1, :]

    count = SOURCES * tiles
    lay_out(0, items[0])

    def step(i, carry):
        n = 2 * i
        lay_out(n + 1, items[1])
        add(n, items[0])
        lay_out(jnp.minimum(n + 2, count - 1), items[0])
        add(n + 1, items[1])
        return carry

    lax.fori_loop(0, count // 2, step, 0)
    side = side_ref[0]

    def finish(c, carry):
        for ref, mine in ((keep_ref, side), (send_ref, 1 - side)):
            start = pl.multiple_of(c * 256 + mine * 128, 128)
            total = accs[0][pl.ds(start, 128), :]
            for acc in accs[1:]:
                total = total + acc[pl.ds(start, 128), :]
            if before is not None:
                total = total + before[0 if ref is keep_ref else 1][c]
            ref[c] = total
        return carry

    lax.fori_loop(0, CODE_ROWS // 256, finish, 0)
    totals_ref[...] = totals if before is None else totals + before[2][...]


def direction_sums(side, at, parts, codes, bins, before):
    owners = CODE_ROWS // 256
    tiles = parts.shape[1]
    arrays = () if before is None else tuple(before)

    def kernel(*refs):
        inputs, rest = refs[: 5 + len(arrays)], refs[5 + len(arrays) :]
        sums_kernel(tiles, before is None, *inputs, *rest)

    return pl.pallas_call(
        kernel,
        out_shape=[
            jax.ShapeDtypeStruct((owners, 128, 128), F32),
            jax.ShapeDtypeStruct((owners, 128, 128), F32),
            jax.ShapeDtypeStruct((8, 128), F32),
        ],
        in_specs=[pl.BlockSpec(memory_space=pltpu.SMEM)] * 2 + vmem(3 + len(arrays)),
        out_specs=vmem(3),
        scratch_shapes=[pltpu.VMEM((128, 128), F32)] * 2
        + [pltpu.VMEM((SOURCES * tiles, 8, 128), F32)]
        + [pltpu.VMEM((CODE_ROWS, 128), F32)] * ACCS,
        cost_estimate=pl.CostEstimate(flops=10**9, bytes_accessed=40 * 10**6, transcendentals=0),
        name="sums",
    )(side, at, parts, codes, bins, *arrays)


def join_kernel(keep_ref, got_ref, totals_ref, other_ref, out_ref):
    out_ref[:, :128] = keep_ref[...] + got_ref[...]
    totals = totals_ref[...] + other_ref[...]
    out_ref[:, 128:] = jnp.broadcast_to(totals[None], (out_ref.shape[0], 8, 128))


def owned_kernel(parts_ref, out_ref):
    total = parts_ref[0]
    for c in range(1, parts_ref.shape[0]):
        total = total + parts_ref[c]
    for z in range(SOURCES):
        out_ref[z, :8] = total[8 * z : 8 * z + 8]
        out_ref[z, 8:] = total[128:]


def finish_kernel(parts_ref, words_ref, levels_ref):
    total = parts_ref[0]
    for z in range(1, SOURCES):
        total = total + parts_ref[z]
    summed = total[:8]
    group = (iota((128, 128), 0) >> 3 == iota((128, 128), 1) >> 3).astype(F32)
    squares = jnp.dot(
        summed * summed, group, precision=lax.Precision.HIGHEST, preferred_element_type=F32
    )
    words = summed / jnp.maximum(jnp.sqrt(squares), 1.0)
    for z in range(SOURCES):
        words_ref[z] = words
    levels_ref[...] = total[8:10] / jnp.maximum(total[10:12], 1.0)


def simple(kernel, name, shapes, *arrays):
    out_shape = [jax.ShapeDtypeStruct(shape, F32) for shape in shapes]
    return pl.pallas_call(
        kernel, out_shape=out_shape, in_specs=vmem(len(arrays)), out_specs=vmem(len(shapes)), name=name
    )(*arrays)


def exchanged(array, axis):
    return lax.all_to_all(array, axis, 0, 0, tiled=True)


def per_device(weights, dir_codes, norm_bins):
    owners = CODE_ROWS // 256
    side = lax.axis_index("row")
    parts, ints = pack(weights, dir_codes, norm_bins)
    parts = parts.reshape(SOURCES, TILES, 8, 128)
    ints = ints.reshape(56, 2, 4, 128).transpose(1, 0, 2, 3).reshape(2, SOURCES, TILES, 128)
    tiles = TILES // CHUNKS
    sums = None
    received = []
    for chunk in range(CHUNKS):
        span = slice(chunk * tiles, (chunk + 1) * tiles)
        gap = jnp.zeros((SOURCES, 16 - tiles, 128), I32)
        lists = jnp.concatenate([ints[0, :, span], gap, ints[1, :, span], gap], axis=1)
        received.append((exchanged(lists, "width"), exchanged(parts[:, span], "width")))
    for lists, chunk_parts in received:
        codes, bins = lists[:, :tiles], lists[:, 16 : 16 + tiles]
        at = (codes >> 4).reshape(-1)
        sums = direction_sums(side.reshape(1), at, chunk_parts, codes, bins, sums)
    keep, send, totals = sums
    swap = [(0, 1), (1, 0)]
    got = lax.ppermute(send, "row", swap)
    other = lax.ppermute(totals, "row", swap)
    (joined,) = simple(join_kernel, "join", [(owners, 136, 128)], keep, got, totals, other)
    joined = exchanged(joined, "cb")
    (owned,) = simple(owned_kernel, "owned", [(SOURCES, 16, 128)], joined)
    owned = exchanged(owned, "width")
    words, levels = simple(finish_kernel, "finish", [(SOURCES, 8, 128), (2, 128)], owned)
    mine = exchanged(words, "width").reshape(128, 128)
    theirs = lax.ppermute(mine, "row", swap)
    first = side == 0
    codewords = jnp.concatenate(
        [jnp.where(first, mine, theirs), jnp.where(first, theirs, mine)], axis=0
    )
    return codewords, levels.reshape(NBINS)


def solution(mesh):
    return jax.shard_map(
        per_device,
        mesh=mesh,
        in_specs=(P(("cb", "row"), "width"),) * 3,
        out_specs=(P("cb", None), P()),
        check_vma=False,
    )
```

```python
import functools
import math

import jax
import jax.numpy as jnp
from jax import lax
from jax.experimental import pallas as pl
from jax.experimental.pallas import tpu as pltpu
from jax.sharding import PartitionSpec as P

WIDTH = 8192
CODES = 65536
NBINS = 256
SCALING = 1.0 / math.sqrt(WIDTH)
F32 = jnp.float32
I32 = jnp.int32

NEAR = 4
FAR = 4
SOURCES = NEAR * FAR
TILES = 14
CHUNKS = (8, 6)
ACCS = 8
CODE_ROWS = CODES // 16


def iota(shape, axis):
    return lax.broadcasted_iota(I32, shape, axis)


def lanes_at(values, index):
    return jnp.take_along_axis(values, index, axis=1, mode="promise_in_bounds")


def vmem(count):
    return [pl.BlockSpec(memory_space=pltpu.VMEM)] * count


def chunk_rows(tiles):
    return -(-10 * tiles // 8) * 8


def pack_kernel(wanted, weights_ref, codes_ref, bins_ref, out, lists_ref):
    common = jnp.bitwise_and(iota((128, 128), 0), iota((128, 128), 1))
    for shift in (4, 2, 1):
        common = jnp.bitwise_xor(common, common >> shift)
    hadamard = (1 - 2 * jnp.bitwise_and(common, 1)).astype(F32).astype(jnp.bfloat16)
    blocks = [
        jnp.dot(weights_ref[:, 128 * b : 128 * b + 128], hadamard, preferred_element_type=F32)
        for b in range(4)
    ]
    sums = [blocks[0] + blocks[1], blocks[0] - blocks[1], blocks[2] + blocks[3], blocks[2] - blocks[3]]
    blocks = [sums[0] + sums[2], sums[1] + sums[3], sums[0] - sums[2], sums[1] - sums[3]]
    lists_ref[:64, :448] = codes_ref[...].astype(F32)
    lists_ref[64:, :448] = bins_ref[...].astype(F32)
    lists = [lists_ref[:, 128 * i : 128 * i + 128].T for i in range(4)]
    lane = iota((8, 128), 1)
    own = jnp.bitwise_and(lane, 7) == iota((8, 128), 0)

    def spread(tile, column):
        block = lists[tile // 16][8 * (tile % 16) : 8 * (tile % 16) + 8, :]
        taken = lanes_at(block, column + (lane >> 3))
        return jnp.sum(jnp.where(own, taken, 0.0), axis=0, keepdims=True)

    for tile in range(56):
        for b in range(4):
            target, t = divmod(4 * tile + b, TILES)
            chunk = 0
            while t >= CHUNKS[chunk]:
                t -= CHUNKS[chunk]
                chunk += 1
            if chunk != wanted:
                continue
            tiles = CHUNKS[chunk]
            out[target, 8 * t : 8 * t + 8, :] = blocks[b][8 * tile : 8 * tile + 8, :]
            out[target, 8 * tiles + t : 8 * tiles + t + 1, :] = spread(tile, 16 * b)
            out[target, 9 * tiles + t : 9 * tiles + t + 1, :] = spread(tile, 64 + 16 * b)


def pack(wanted, weights, codes, bins):
    return pl.pallas_call(
        functools.partial(pack_kernel, wanted),
        out_shape=jax.ShapeDtypeStruct((SOURCES, chunk_rows(CHUNKS[wanted]), 128), F32),
        in_specs=vmem(3),
        out_specs=pl.BlockSpec(memory_space=pltpu.VMEM),
        cost_estimate=pl.CostEstimate(flops=10**9, bytes_accessed=2 * 10**6, transcendentals=0),
        scratch_shapes=[pltpu.VMEM((128, 512), F32)],
        name="pack",
    )(weights, codes, bins)


def sums_kernel(tiles, first, *refs):
    side_ref, parts_ref = refs[:2]
    before = refs[2:4] if not first else (None, None)
    keep_ref, send_ref, at_ref, at_sem, codes_ref, directions_ref = refs[-8 - ACCS : -2 - ACCS]
    items, accs = refs[-2 - ACCS : -ACCS], refs[-ACCS:]
    lane = iota((8, 128), 1)
    place = iota((8, 128), 0)
    inner = jnp.bitwise_and(lane, 7)
    outer = lane >> 3
    for h in range(SOURCES):
        codes_ref[h * tiles : (h + 1) * tiles, :] = parts_ref[h, 8 * tiles : 9 * tiles, :].astype(I32) >> 4
    fetch = pltpu.make_async_copy(codes_ref, at_ref, at_sem)
    fetch.start()
    for acc in accs:
        acc[...] = jnp.zeros_like(acc)
    group = (iota((128, 128), 0) >> 3 == iota((128, 128), 1) >> 3).astype(F32)

    def rotate(t, carry):
        z = [parts_ref[h, pl.ds(pl.multiple_of(8 * t, 8), 8), :] for h in range(SOURCES)]
        for bit in range(4):
            d = 1 << bit
            z = [z[h ^ d] - z[h] if h & d else z[h] + z[h ^ d] for h in range(SOURCES)]
        rotated = jnp.concatenate(z, axis=0) * SCALING
        squares = jnp.dot(
            rotated * rotated, group, precision=lax.Precision.HIGHEST, preferred_element_type=F32
        )
        floored = jnp.maximum(jnp.sqrt(squares), 1.0)
        directions = rotated / floored
        logs = jnp.log(floored)
        packed = []
        for half in range(2):
            log_sum = jnp.zeros((8, 128), F32)
            bin_sum = jnp.zeros((8, 128), I32)
            for j in range(8):
                h = 8 * half + j
                bins = jnp.broadcast_to(parts_ref[h, pl.ds(9 * tiles + t, 1), :], (8, 128)).astype(I32)
                bins = lanes_at(bins, 8 * outer + place)
                log_sum = log_sum + jnp.where(inner == j, logs[8 * h : 8 * h + 8], 0.0)
                bin_sum = bin_sum + jnp.where(inner == j, bins, 0)
            packed.append((log_sum, bin_sum))
        for h in range(SOURCES):
            directions_ref[h * tiles + t] = directions[8 * h : 8 * h + 8]
        base = packed[0][1] >> 4
        low, high, low_count, high_count = carry
        for offset in range(16):
            log_total = jnp.zeros((8, 128), F32)
            count = jnp.zeros((8, 128), F32)
            for log_sum, bin_sum in packed:
                chosen = jnp.bitwise_and(bin_sum, 15) == offset
                log_total = log_total + jnp.where(chosen, log_sum, 0.0)
                count = count + jnp.where(chosen, 1.0, 0.0)
            log_total = jnp.sum(log_total, axis=1, keepdims=True)
            count = jnp.sum(count, axis=1, keepdims=True)
            target = 16 * base + offset
            at_low, at_high = target == lane, target == lane + 128
            low = low + jnp.where(at_low, log_total, 0.0)
            high = high + jnp.where(at_high, log_total, 0.0)
            low_count = low_count + jnp.where(at_low, count, 0.0)
            high_count = high_count + jnp.where(at_high, count, 0.0)
        return low, high, low_count, high_count

    empty = jnp.zeros((8, 128), F32)
    bin_parts = lax.fori_loop(0, tiles, rotate, (empty,) * 4)
    rows = [jnp.sum(part, axis=0, keepdims=True) for part in bin_parts]
    totals = jnp.concatenate(rows + [jnp.zeros((4, 128), F32)], axis=0)

    def lay_out(n, items_ref):
        h, t = n // tiles, n % tiles
        direction = directions_ref[n]
        codes = jnp.broadcast_to(parts_ref[h, pl.ds(8 * tiles + t, 1), :], (8, 128)).astype(I32)
        codes = jnp.bitwise_and(codes, 15)
        for k in range(16):
            values = lanes_at(direction, 8 * k + inner)
            slot = lanes_at(codes, 8 * k + place)
            items_ref[8 * k : 8 * k + 8, :] = jnp.where(slot == outer, values, 0.0)

    def add(n, items_ref):
        for k in range(16):
            at = [at_ref[n, 8 * k + s] for s in range(ACCS)]
            old = [accs[s][pl.ds(at[s], 1), :] for s in range(ACCS)]
            for s in range(ACCS):
                accs[s][pl.ds(at[s], 1), :] = old[s] + items_ref[8 * k + s : 8 * k + s + 1, :]

    count = SOURCES * tiles
    fetch.wait()
    lay_out(0, items[0])

    def step(i, carry):
        n = 2 * i
        lay_out(n + 1, items[1])
        add(n, items[0])
        lay_out(jnp.minimum(n + 2, count - 1), items[0])
        add(n + 1, items[1])
        return carry

    lax.fori_loop(0, count // 2, step, 0)
    side = side_ref[0]

    def finish(c, carry):
        for ref, earlier, mine in ((keep_ref, before[0], side), (send_ref, before[1], 1 - side)):
            for near in range(NEAR):
                start = pl.multiple_of(c * 256 + near * 64 + mine * 32, 32)
                total = accs[0][pl.ds(start, 32), :]
                for acc in accs[1:]:
                    total = total + acc[pl.ds(start, 32), :]
                rows = slice(32 * near, 32 * near + 32)
                ref[c, rows] = total if first else total + earlier[c, rows]
            ref[c, 128:] = totals if first else totals + earlier[c, 128:]
        return carry

    lax.fori_loop(0, CODE_ROWS // 256, finish, 0)


def direction_sums(side, parts, tiles, before):
    owners = CODE_ROWS // 256
    arrays = () if before is None else tuple(before)

    def kernel(*refs):
        sums_kernel(tiles, before is None, *refs)

    return pl.pallas_call(
        kernel,
        out_shape=[jax.ShapeDtypeStruct((owners, 136, 128), F32)] * 2,
        in_specs=[pl.BlockSpec(memory_space=pltpu.SMEM)] + vmem(1 + len(arrays)),
        out_specs=vmem(2),
        scratch_shapes=[
            pltpu.SMEM((SOURCES * tiles, 128), I32),
            pltpu.SemaphoreType.DMA,
            pltpu.VMEM((SOURCES * tiles, 128), I32),
            pltpu.VMEM((SOURCES * tiles, 8, 128), F32),
        ]
        + [pltpu.VMEM((128, 128), F32)] * 2
        + [pltpu.VMEM((CODE_ROWS, 128), F32)] * ACCS,
        cost_estimate=pl.CostEstimate(
            flops=2 * 10**9 * tiles, bytes_accessed=4 * 10**6 * tiles, transcendentals=0
        ),
        name="sums",
    )(side, parts, *arrays)


def summed(parts_ref):
    total = parts_ref[0]
    for i in range(1, parts_ref.shape[0]):
        total = total + parts_ref[i]
    return total


def owned_kernel(parts_ref, out_ref):
    total = summed(parts_ref)
    for near in range(NEAR):
        out_ref[near, :32] = total[32 * near : 32 * near + 32]
        out_ref[near, 32:] = total[128:]


def spread_kernel(parts_ref, out_ref):
    out_ref[...] = jnp.broadcast_to(summed(parts_ref)[None], out_ref.shape)


def finish_kernel(parts_ref, words_ref, levels_ref):
    total = summed(parts_ref)
    sums = total[:32]
    group = (iota((128, 128), 0) >> 3 == iota((128, 128), 1) >> 3).astype(F32)
    squares = jnp.dot(sums * sums, group, precision=lax.Precision.HIGHEST, preferred_element_type=F32)
    words = sums / jnp.maximum(jnp.sqrt(squares), 1.0)
    words_ref[...] = jnp.broadcast_to(words[None], words_ref.shape)
    levels_ref[...] = total[32:34] / jnp.maximum(total[34:36], 1.0)


def simple(kernel, name, shapes, *arrays):
    out_shape = [jax.ShapeDtypeStruct(shape, F32) for shape in shapes]
    return pl.pallas_call(
        kernel, out_shape=out_shape, in_specs=vmem(len(arrays)), out_specs=vmem(len(shapes)), name=name
    )(*arrays)


def exchanged(array, axis):
    return lax.all_to_all(array, axis, 0, 0, tiled=True)


def per_device(weights, dir_codes, norm_bins):
    side = lax.axis_index("row")
    received = [
        exchanged(pack(chunk, weights, dir_codes.T, norm_bins.T), ("far", "near"))
        for chunk in range(len(CHUNKS))
    ]
    sums = None
    for chunk, tiles in zip(received, CHUNKS):
        sums = direction_sums(side.reshape(1), chunk, tiles, sums)
    keep, send = sums
    joined = exchanged(keep + lax.ppermute(send, "row", [(0, 1), (1, 0)]), "cb")
    (owned,) = simple(owned_kernel, "owned", [(NEAR, 40, 128)], joined)
    (owned,) = simple(spread_kernel, "spread", [(FAR, 40, 128)], exchanged(owned, "near"))
    words, levels = simple(
        finish_kernel, "finish", [(2 * NEAR, 32, 128), (2, 128)], exchanged(owned, "far")
    )
    codewords = exchanged(words, ("near", "row"))
    return codewords.reshape(256, 128), levels.reshape(NBINS)


def solution(mesh):
    names = {"width": ("far", "near"), "cb": ("cb",), "row": ("row",)}
    sizes = {"far": FAR, "near": NEAR, "cb": mesh.shape["cb"], "row": mesh.shape["row"]}
    axes = tuple(part for name in mesh.axis_names for part in names[name])
    fine = jax.sharding.Mesh(mesh.devices.reshape([sizes[axis] for axis in axes]), axes)
    spec = P(("cb", "row"), ("far", "near"))
    return jax.shard_map(
        per_device,
        mesh=fine,
        in_specs=(spec,) * 3,
        out_specs=(P("cb", None), P()),
        check_vma=False,
    )
```

```python
import functools
import math

import jax
import jax.numpy as jnp
from jax import lax
from jax.experimental import pallas as pl
from jax.experimental.pallas import tpu as pltpu
from jax.sharding import PartitionSpec as P

WIDTH = 8192
CODES = 65536
NBINS = 256
SCALING = 1.0 / math.sqrt(WIDTH)
F32 = jnp.float32
I32 = jnp.int32

NEAR = 2
FAR = 8
PIECE = 128 // NEAR
SOURCES = NEAR * FAR
TILES = 14
CHUNKS = (8, 6)
ACCS = 8
ITEMS = 4
SCRATCH = 2 + 3 * ACCS + ITEMS
CODE_ROWS = CODES // 16


def iota(shape, axis):
    return lax.broadcasted_iota(I32, shape, axis)


def lanes_at(values, index):
    return jnp.take_along_axis(values, index, axis=1, mode="promise_in_bounds")


def vmem(count):
    return [pl.BlockSpec(memory_space=pltpu.VMEM)] * count


def chunk_rows(tiles):
    return -(-10 * tiles // 8) * 8


def pack_kernel(wanted, weights_ref, codes_ref, bins_ref, out, lists_ref):
    common = jnp.bitwise_and(iota((128, 128), 0), iota((128, 128), 1))
    for shift in (4, 2, 1):
        common = jnp.bitwise_xor(common, common >> shift)
    hadamard = (1 - 2 * jnp.bitwise_and(common, 1)).astype(F32).astype(jnp.bfloat16)
    blocks = [
        jnp.dot(weights_ref[:, 128 * b : 128 * b + 128], hadamard, preferred_element_type=F32)
        for b in range(4)
    ]
    sums = [blocks[0] + blocks[1], blocks[0] - blocks[1], blocks[2] + blocks[3], blocks[2] - blocks[3]]
    blocks = [sums[0] + sums[2], sums[1] + sums[3], sums[0] - sums[2], sums[1] - sums[3]]
    lists_ref[:64, :448] = codes_ref[...].astype(F32)
    lists_ref[64:, :448] = bins_ref[...].astype(F32)
    lists = [lists_ref[:, 128 * i : 128 * i + 128].T for i in range(4)]
    lane = iota((8, 128), 1)
    own = jnp.bitwise_and(lane, 7) == iota((8, 128), 0)

    def spread(tile, column):
        block = lists[tile // 16][8 * (tile % 16) : 8 * (tile % 16) + 8, :]
        taken = lanes_at(block, column + (lane >> 3))
        return jnp.sum(jnp.where(own, taken, 0.0), axis=0, keepdims=True)

    for tile in range(56):
        for b in range(4):
            target, t = divmod(4 * tile + b, TILES)
            chunk = 0
            while t >= CHUNKS[chunk]:
                t -= CHUNKS[chunk]
                chunk += 1
            if chunk != wanted:
                continue
            tiles = CHUNKS[chunk]
            out[target, 8 * t : 8 * t + 8, :] = blocks[b][8 * tile : 8 * tile + 8, :]
            out[target, 8 * tiles + t : 8 * tiles + t + 1, :] = spread(tile, 16 * b)
            out[target, 9 * tiles + t : 9 * tiles + t + 1, :] = spread(tile, 64 + 16 * b)


def pack(wanted, weights, codes, bins):
    return pl.pallas_call(
        functools.partial(pack_kernel, wanted),
        out_shape=jax.ShapeDtypeStruct((SOURCES, chunk_rows(CHUNKS[wanted]), 128), F32),
        in_specs=vmem(3),
        out_specs=pl.BlockSpec(memory_space=pltpu.VMEM),
        cost_estimate=pl.CostEstimate(flops=10**9, bytes_accessed=2 * 10**6, transcendentals=0),
        scratch_shapes=[pltpu.VMEM((128, 512), F32)],
        name="pack",
    )(weights, codes, bins)


def sums_kernel(tiles, first, *refs):
    side_ref, parts_ref = refs[:2]
    inputs = 2 if first else 4
    keep_ref, send_ref = refs[inputs : inputs + 2]
    scratch = refs[inputs + 2 : inputs + 2 + SCRATCH]
    loads = []
    before = refs[inputs + 2 + SCRATCH :]
    if not first:
        sums_sems, before = before[0], before[1:]
        loads = [pltpu.make_async_copy(refs[2 + i], before[i], sums_sems.at[i]) for i in range(2)]
        for load in loads:
            load.start()
    at_sems, directions_ref = scratch[0], scratch[1]
    rows_refs, at_refs = scratch[2 : 2 + ACCS], scratch[2 + ACCS : 2 + 2 * ACCS]
    accs, items = scratch[2 + 2 * ACCS : 2 + 3 * ACCS], scratch[2 + 3 * ACCS :]
    lane = iota((8, 128), 1)
    place = iota((8, 128), 0)
    inner = jnp.bitwise_and(lane, 7)
    outer = lane >> 3
    for t in range(tiles):
        for h in range(SOURCES):
            row = parts_ref[h, 8 * tiles + t : 8 * tiles + t + 1, :].astype(I32) >> 4
            m = 2 * t + h // ACCS
            rows_refs[h % ACCS][m : m + 1, :] = row
    fetches = [
        pltpu.make_async_copy(rows_refs[j], at_refs[j], at_sems.at[j]) for j in range(ACCS)
    ]
    for fetch in fetches:
        fetch.start()
    share = -(-CODE_ROWS // (8 * tiles))
    group = (iota((128, 128), 0) >> 3 == iota((128, 128), 1) >> 3).astype(F32)

    def clear(t, offset):
        start = jnp.minimum(t * share, CODE_ROWS // 8 - share)
        for i in range(offset, share, 16):
            for acc in accs:
                acc[pl.ds(pl.multiple_of(8 * (start + i), 8), 8), :] = jnp.zeros((8, 128), F32)

    def rotate(t, carry):
        z = [parts_ref[h, pl.ds(pl.multiple_of(8 * t, 8), 8), :] for h in range(SOURCES)]
        for bit in range(4):
            d = 1 << bit
            z = [z[h ^ d] - z[h] if h & d else z[h] + z[h ^ d] for h in range(SOURCES)]
        rotated = jnp.concatenate(z, axis=0) * SCALING
        squares = jnp.dot(
            rotated * rotated, group, precision=lax.Precision.HIGHEST, preferred_element_type=F32
        )
        floored = jnp.maximum(jnp.sqrt(squares), 1.0)
        directions = rotated / floored
        logs = jnp.log(floored)
        packed = []
        for half in range(2):
            log_sum = jnp.zeros((8, 128), F32)
            bin_sum = jnp.zeros((8, 128), I32)
            for j in range(8):
                h = 8 * half + j
                bins = jnp.broadcast_to(parts_ref[h, pl.ds(9 * tiles + t, 1), :], (8, 128)).astype(I32)
                bins = lanes_at(bins, 8 * outer + place)
                log_sum = log_sum + jnp.where(inner == j, logs[8 * h : 8 * h + 8], 0.0)
                bin_sum = bin_sum + jnp.where(inner == j, bins, 0)
            packed.append((log_sum, bin_sum))
        for h in range(SOURCES):
            directions_ref[SOURCES * t + h] = directions[8 * h : 8 * h + 8]
        base = packed[0][1] >> 4
        low, high, low_count, high_count = carry
        for offset in range(16):
            clear(t, offset)
            log_total = jnp.zeros((8, 128), F32)
            count = jnp.zeros((8, 128), F32)
            for log_sum, bin_sum in packed:
                chosen = jnp.bitwise_and(bin_sum, 15) == offset
                log_total = log_total + jnp.where(chosen, log_sum, 0.0)
                count = count + jnp.where(chosen, 1.0, 0.0)
            log_total = jnp.sum(log_total, axis=1, keepdims=True)
            count = jnp.sum(count, axis=1, keepdims=True)
            target = 16 * base + offset
            at_low, at_high = target == lane, target == lane + 128
            low = low + jnp.where(at_low, log_total, 0.0)
            high = high + jnp.where(at_high, log_total, 0.0)
            low_count = low_count + jnp.where(at_low, count, 0.0)
            high_count = high_count + jnp.where(at_high, count, 0.0)
        return low, high, low_count, high_count

    empty = jnp.zeros((8, 128), F32)
    bin_parts = lax.fori_loop(0, tiles, rotate, (empty,) * 4)
    rows = [jnp.sum(part, axis=0, keepdims=True) for part in bin_parts]
    totals = jnp.concatenate(rows + [jnp.zeros((4, 128), F32)], axis=0)

    for fetch in fetches:
        fetch.wait()

    def step(m, carry):
        t, half = m >> 1, jnp.bitwise_and(m, 1)
        moved = [directions_ref[ACCS * m + j] for j in range(ACCS)]
        slots = []
        for j in range(ACCS):
            row = parts_ref[ACCS * half + j, pl.ds(8 * tiles + t, 1), :]
            slots.append(jnp.bitwise_and(jnp.broadcast_to(row, (8, 128)).astype(I32), 15))
        for k in range(16):
            items_ref = items[k % len(items)]
            for j in range(ACCS):
                values = lanes_at(moved[j], 8 * k + inner)
                slot = lanes_at(slots[j], 8 * k + place)
                items_ref[8 * j : 8 * j + 8, :] = jnp.where(slot == outer, values, 0.0)
            for s in range(8):
                at = [at_refs[j][m, 8 * k + s] for j in range(ACCS)]
                old = [accs[j][pl.ds(at[j], 1), :] for j in range(ACCS)]
                for j in range(ACCS):
                    accs[j][pl.ds(at[j], 1), :] = old[j] + items_ref[8 * j + s : 8 * j + s + 1, :]
        return carry

    lax.fori_loop(0, 2 * tiles, step, 0)
    side = side_ref[0]

    owners = CODE_ROWS // 256
    for load in loads:
        load.wait()

    def finish(c, carry):
        for i, ref, mine in ((0, keep_ref, side), (1, send_ref, 1 - side)):
            for near in range(NEAR):
                start = pl.multiple_of(c * 256 + (2 * near + mine) * PIECE, PIECE)
                total = accs[0][pl.ds(start, PIECE), :]
                for acc in accs[1:]:
                    total = total + acc[pl.ds(start, PIECE), :]
                to = near * owners + c
                ref[to, :PIECE] = total if first else total + before[i][to, :PIECE]
                ref[to, PIECE:] = totals if first else totals + before[i][to, PIECE:]
        return carry

    lax.fori_loop(0, owners, finish, 0)


def direction_sums(side, parts, tiles, before):
    shape = (NEAR * CODE_ROWS // 256, PIECE + 8, 128)
    arrays = () if before is None else tuple(before)

    def kernel(*refs):
        sums_kernel(tiles, before is None, *refs)

    return pl.pallas_call(
        kernel,
        out_shape=[jax.ShapeDtypeStruct(shape, F32)] * 2,
        in_specs=[pl.BlockSpec(memory_space=pltpu.SMEM)]
        + vmem(1)
        + [pl.BlockSpec(memory_space=pl.ANY)] * len(arrays),
        out_specs=vmem(2),
        scratch_shapes=[
            pltpu.SemaphoreType.DMA((ACCS,)),
            pltpu.VMEM((SOURCES * tiles, 8, 128), F32),
        ]
        + [pltpu.VMEM((2 * tiles, 128), I32)] * ACCS
        + [pltpu.SMEM((2 * tiles, 128), I32)] * ACCS
        + [pltpu.VMEM((CODE_ROWS, 128), F32)] * ACCS
        + [pltpu.VMEM((8 * ACCS, 128), F32)] * ITEMS
        + ([] if before is None else [pltpu.SemaphoreType.DMA((2,))] + [pltpu.VMEM(shape, F32)] * 2),
        cost_estimate=pl.CostEstimate(
            flops=2 * 10**9 * tiles, bytes_accessed=4 * 10**6 * tiles, transcendentals=0
        ),
        name="sums",
    )(side, parts, *arrays)


def summed(parts_ref):
    total = parts_ref[0]
    for i in range(1, parts_ref.shape[0]):
        total = total + parts_ref[i]
    return total


def owned_kernel(parts_ref, out_ref):
    out_ref[...] = jnp.broadcast_to(summed(parts_ref)[None], out_ref.shape)


def finish_kernel(parts_ref, words_ref, levels_ref):
    total = summed(parts_ref)
    sums = total[:PIECE]
    group = (iota((128, 128), 0) >> 3 == iota((128, 128), 1) >> 3).astype(F32)
    squares = jnp.dot(sums * sums, group, precision=lax.Precision.HIGHEST, preferred_element_type=F32)
    words = sums / jnp.maximum(jnp.sqrt(squares), 1.0)
    words_ref[...] = jnp.broadcast_to(words[None], words_ref.shape)
    levels_ref[...] = total[PIECE : PIECE + 2] / jnp.maximum(total[PIECE + 2 : PIECE + 4], 1.0)


def simple(kernel, name, shapes, *arrays):
    out_shape = [jax.ShapeDtypeStruct(shape, F32) for shape in shapes]
    return pl.pallas_call(
        kernel, out_shape=out_shape, in_specs=vmem(len(arrays)), out_specs=vmem(len(shapes)), name=name
    )(*arrays)


def exchanged(array, axis):
    return lax.all_to_all(array, axis, 0, 0, tiled=True)


def per_device(weights, dir_codes, norm_bins):
    side = lax.axis_index("row")
    received = [
        exchanged(pack(chunk, weights, dir_codes.T, norm_bins.T), ("far", "near"))
        for chunk in range(len(CHUNKS))
    ]
    sums = None
    for chunk, tiles in zip(received, CHUNKS):
        sums = direction_sums(side.reshape(1), chunk, tiles, sums)
    keep, send = sums
    joined = exchanged(keep + lax.ppermute(send, "row", [(0, 1), (1, 0)]), ("near", "cb"))
    (owned,) = simple(owned_kernel, "owned", [(FAR, PIECE + 8, 128)], joined)
    words, levels = simple(
        finish_kernel, "finish", [(2 * NEAR, PIECE, 128), (2, 128)], exchanged(owned, "far")
    )
    codewords = exchanged(words, ("near", "row"))
    return codewords.reshape(256, 128), levels.reshape(NBINS)


def solution(mesh):
    names = {"width": ("far", "near"), "cb": ("cb",), "row": ("row",)}
    sizes = {"far": FAR, "near": NEAR, "cb": mesh.shape["cb"], "row": mesh.shape["row"]}
    axes = tuple(part for name in mesh.axis_names for part in names[name])
    fine = jax.sharding.Mesh(mesh.devices.reshape([sizes[axis] for axis in axes]), axes)
    spec = P(("cb", "row"), ("far", "near"))
    return jax.shard_map(
        per_device,
        mesh=fine,
        in_specs=(spec,) * 3,
        out_specs=(P("cb", None), P()),
        check_vma=False,
    )
```

```python
import functools
import math

import jax
import jax.numpy as jnp
from jax import lax
from jax.experimental import pallas as pl
from jax.experimental.pallas import tpu as pltpu
from jax.sharding import PartitionSpec as P

WIDTH = 8192
CODES = 65536
NBINS = 256
SCALING = 1.0 / math.sqrt(WIDTH)
F32 = jnp.float32
I32 = jnp.int32

NEAR = 2
FAR = 8
PIECE = 128 // NEAR
SOURCES = NEAR * FAR
TILES = 14
CHUNKS = (9, 5)
BINNED = (7, 7)
LATE = CHUNKS[0] - BINNED[0]
ACCS = 8
ITEMS = 4
SCRATCH = 4 + 3 * ACCS + ITEMS
CODE_ROWS = CODES // 16


def iota(shape, axis):
    return lax.broadcasted_iota(I32, shape, axis)


def lanes_at(values, index):
    return jnp.take_along_axis(values, index, axis=1, mode="promise_in_bounds")


def vmem(count):
    return [pl.BlockSpec(memory_space=pltpu.VMEM)] * count


def chunk_rows(chunk):
    return -(-(9 * CHUNKS[chunk] + BINNED[chunk]) // 8) * 8


def place_in(counts, t):
    chunk = 0
    while t >= counts[chunk]:
        t -= counts[chunk]
        chunk += 1
    return chunk, t


def pack_kernel(wanted, weights_ref, codes_ref, bins_ref, out, lists_ref):
    common = jnp.bitwise_and(iota((128, 128), 0), iota((128, 128), 1))
    for shift in (4, 2, 1):
        common = jnp.bitwise_xor(common, common >> shift)
    hadamard = (1 - 2 * jnp.bitwise_and(common, 1)).astype(F32).astype(jnp.bfloat16)
    blocks = [
        jnp.dot(weights_ref[:, 128 * b : 128 * b + 128], hadamard, preferred_element_type=F32)
        for b in range(4)
    ]
    sums = [blocks[0] + blocks[1], blocks[0] - blocks[1], blocks[2] + blocks[3], blocks[2] - blocks[3]]
    blocks = [sums[0] + sums[2], sums[1] + sums[3], sums[0] - sums[2], sums[1] - sums[3]]
    lists_ref[:64, :448] = codes_ref[...].astype(F32)
    lists_ref[64:, :448] = bins_ref[...].astype(F32)
    lists = [lists_ref[:, 128 * i : 128 * i + 128].T for i in range(4)]
    lane = iota((8, 128), 1)
    own = jnp.bitwise_and(lane, 7) == iota((8, 128), 0)

    def spread(tile, column):
        block = lists[tile // 16][8 * (tile % 16) : 8 * (tile % 16) + 8, :]
        taken = lanes_at(block, column + (lane >> 3))
        return jnp.sum(jnp.where(own, taken, 0.0), axis=0, keepdims=True)

    for tile in range(56):
        for b in range(4):
            target, t = divmod(4 * tile + b, TILES)
            chunk, at = place_in(CHUNKS, t)
            tiles = CHUNKS[chunk]
            if chunk == wanted:
                out[target, 8 * at : 8 * at + 8, :] = blocks[b][8 * tile : 8 * tile + 8, :]
                out[target, 8 * tiles + at : 8 * tiles + at + 1, :] = spread(tile, 16 * b)
            chunk, at = place_in(BINNED, t)
            at += 9 * CHUNKS[chunk]
            if chunk == wanted:
                out[target, at : at + 1, :] = spread(tile, 64 + 16 * b)


def pack(wanted, weights, codes, bins):
    return pl.pallas_call(
        functools.partial(pack_kernel, wanted),
        out_shape=jax.ShapeDtypeStruct((SOURCES, chunk_rows(wanted), 128), F32),
        in_specs=vmem(3),
        out_specs=pl.BlockSpec(memory_space=pltpu.VMEM),
        cost_estimate=pl.CostEstimate(flops=10**9, bytes_accessed=2 * 10**6, transcendentals=0),
        scratch_shapes=[pltpu.VMEM((128, 512), F32)],
        name="pack",
    )(weights, codes, bins)


def sums_kernel(chunk, *refs):
    tiles, binned, first = CHUNKS[chunk], BINNED[chunk], chunk == 0
    inputs = 2 if first else 5
    outputs = 3 if first else 2
    side_ref, sent_ref = refs[:2]
    keep_ref, send_ref = refs[inputs : inputs + 2]
    scratch = refs[inputs + outputs :]
    at_sems, directions_ref, parts_ref, part_sem = scratch[:4]
    rows_refs, at_refs = scratch[4 : 4 + ACCS], scratch[4 + ACCS : 4 + 2 * ACCS]
    accs, items = scratch[4 + 2 * ACCS : 4 + 3 * ACCS], scratch[4 + 3 * ACCS : SCRATCH]
    arrival = pltpu.make_async_copy(sent_ref, parts_ref, part_sem)
    arrival.start()
    loads = []
    before = scratch[SCRATCH:]
    if not first:
        sums_sems, before = before[0], before[1:]
        loads = [pltpu.make_async_copy(refs[2 + i], before[i], sums_sems.at[i]) for i in range(2)]
        for load in loads:
            load.start()
    arrival.wait()
    lane = iota((8, 128), 1)
    place = iota((8, 128), 0)
    inner = jnp.bitwise_and(lane, 7)
    outer = lane >> 3
    for t in range(tiles):
        for h in range(SOURCES):
            row = parts_ref[h, 8 * tiles + t : 8 * tiles + t + 1, :].astype(I32) >> 4
            m = 2 * t + h // ACCS
            rows_refs[h % ACCS][m : m + 1, :] = row
    fetches = [
        pltpu.make_async_copy(rows_refs[j], at_refs[j], at_sems.at[j]) for j in range(ACCS)
    ]
    for fetch in fetches:
        fetch.start()
    share = -(-CODE_ROWS // (8 * tiles))
    group = (iota((128, 128), 0) >> 3 == iota((128, 128), 1) >> 3).astype(F32)

    def clear(t, offset):
        start = jnp.minimum(t * share, CODE_ROWS // 8 - share)
        for i in range(offset, share, 16):
            for acc in accs:
                acc[pl.ds(pl.multiple_of(8 * (start + i), 8), 8), :] = jnp.zeros((8, 128), F32)

    def bins_of(row):
        sums = []
        for half in range(2):
            bin_sum = jnp.zeros((8, 128), I32)
            for j in range(8):
                bins = parts_ref[8 * half + j, pl.ds(9 * tiles + row, 1), :]
                bins = lanes_at(jnp.broadcast_to(bins, (8, 128)).astype(I32), 8 * outer + place)
                bin_sum = bin_sum + jnp.where(inner == j, bins, 0)
            sums.append(bin_sum)
        return sums

    def counted(log_sums, bin_sums, carry):
        base = bin_sums[0] >> 4
        low, high, low_count, high_count = carry
        for offset in range(16):
            log_total = jnp.zeros((8, 128), F32)
            count = jnp.zeros((8, 128), F32)
            for log_sum, bin_sum in zip(log_sums, bin_sums):
                chosen = jnp.bitwise_and(bin_sum, 15) == offset
                log_total = log_total + jnp.where(chosen, log_sum, 0.0)
                count = count + jnp.where(chosen, 1.0, 0.0)
            log_total = jnp.sum(log_total, axis=1, keepdims=True)
            count = jnp.sum(count, axis=1, keepdims=True)
            target = 16 * base + offset
            at_low, at_high = target == lane, target == lane + 128
            low = low + jnp.where(at_low, log_total, 0.0)
            high = high + jnp.where(at_high, log_total, 0.0)
            low_count = low_count + jnp.where(at_low, count, 0.0)
            high_count = high_count + jnp.where(at_high, count, 0.0)
        return low, high, low_count, high_count

    def rotate(t):
        z = [parts_ref[h, pl.ds(pl.multiple_of(8 * t, 8), 8), :] for h in range(SOURCES)]
        for bit in range(4):
            d = 1 << bit
            z = [z[h ^ d] - z[h] if h & d else z[h] + z[h ^ d] for h in range(SOURCES)]
        rotated = jnp.concatenate(z, axis=0) * SCALING
        squares = jnp.dot(
            rotated * rotated, group, precision=lax.Precision.HIGHEST, preferred_element_type=F32
        )
        floored = jnp.maximum(jnp.sqrt(squares), 1.0)
        directions = rotated / floored
        logs = jnp.log(floored)
        for h in range(SOURCES):
            directions_ref[SOURCES * t + h] = directions[8 * h : 8 * h + 8]
        for offset in range(16):
            clear(t, offset)
        sums = []
        for half in range(2):
            log_sum = jnp.zeros((8, 128), F32)
            for j in range(8):
                h = 8 * half + j
                log_sum = log_sum + jnp.where(inner == j, logs[8 * h : 8 * h + 8], 0.0)
            sums.append(log_sum)
        return sums

    def rotate_and_count(t, carry):
        bin_sums = bins_of(t if first else t + LATE)
        return counted(rotate(t), bin_sums, carry)

    empty = jnp.zeros((8, 128), F32)
    bin_parts = (empty,) * 4
    if first:
        for t in range(binned, tiles):
            for half, log_sum in enumerate(rotate(t)):
                refs[inputs + 2][2 * (t - binned) + half] = log_sum
    else:
        for row in range(LATE):
            late = [refs[4][2 * row + half] for half in range(2)]
            bin_parts = counted(late, bins_of(row), bin_parts)
    bin_parts = lax.fori_loop(0, min(tiles, binned), rotate_and_count, bin_parts)
    rows = [jnp.sum(part, axis=0, keepdims=True) for part in bin_parts]
    totals = jnp.concatenate(rows + [jnp.zeros((4, 128), F32)], axis=0)

    for fetch in fetches:
        fetch.wait()

    def step(m, carry):
        t, half = m >> 1, jnp.bitwise_and(m, 1)
        moved = [directions_ref[ACCS * m + j] for j in range(ACCS)]
        slots = []
        for j in range(ACCS):
            row = parts_ref[ACCS * half + j, pl.ds(8 * tiles + t, 1), :]
            slots.append(jnp.bitwise_and(jnp.broadcast_to(row, (8, 128)).astype(I32), 15))
        for k in range(16):
            items_ref = items[k % len(items)]
            for j in range(ACCS):
                values = lanes_at(moved[j], 8 * k + inner)
                slot = lanes_at(slots[j], 8 * k + place)
                items_ref[8 * j : 8 * j + 8, :] = jnp.where(slot == outer, values, 0.0)
            for s in range(8):
                at = [at_refs[j][m, 8 * k + s] for j in range(ACCS)]
                old = [accs[j][pl.ds(at[j], 1), :] for j in range(ACCS)]
                for j in range(ACCS):
                    accs[j][pl.ds(at[j], 1), :] = old[j] + items_ref[8 * j + s : 8 * j + s + 1, :]
        return carry

    lax.fori_loop(0, 2 * tiles, step, 0)
    side = side_ref[0]

    owners = CODE_ROWS // 256
    for load in loads:
        load.wait()

    def finish(c, carry):
        for i, ref, mine in ((0, keep_ref, side), (1, send_ref, 1 - side)):
            for near in range(NEAR):
                start = pl.multiple_of(c * 256 + (2 * near + mine) * PIECE, PIECE)
                total = accs[0][pl.ds(start, PIECE), :]
                for acc in accs[1:]:
                    total = total + acc[pl.ds(start, PIECE), :]
                to = near * owners + c
                ref[to, :PIECE] = total if first else total + before[i][to, :PIECE]
                ref[to, PIECE:] = totals if first else totals + before[i][to, PIECE:]
        return carry

    lax.fori_loop(0, owners, finish, 0)


def direction_sums(side, parts, chunk, before):
    tiles, shape = CHUNKS[chunk], (NEAR * CODE_ROWS // 256, PIECE + 8, 128)
    arrays = () if before is None else tuple(before)
    later = [pltpu.SemaphoreType.DMA((2,))] + [pltpu.VMEM(shape, F32)] * 2
    anywhere = pl.BlockSpec(memory_space=pl.ANY)
    logs = [jax.ShapeDtypeStruct((2 * LATE, 8, 128), F32)]
    return pl.pallas_call(
        functools.partial(sums_kernel, chunk),
        out_shape=[jax.ShapeDtypeStruct(shape, F32)] * 2 + (logs if before is None else []),
        in_specs=[pl.BlockSpec(memory_space=pltpu.SMEM), anywhere]
        + ([] if before is None else [anywhere] * 2 + vmem(1)),
        out_specs=vmem(3 if before is None else 2),
        scratch_shapes=[
            pltpu.SemaphoreType.DMA((ACCS,)),
            pltpu.VMEM((SOURCES * tiles, 8, 128), F32),
            pltpu.VMEM(parts.shape, F32),
            pltpu.SemaphoreType.DMA,
        ]
        + [pltpu.VMEM((2 * tiles, 128), I32)] * ACCS
        + [pltpu.SMEM((2 * tiles, 128), I32)] * ACCS
        + [pltpu.VMEM((CODE_ROWS, 128), F32)] * ACCS
        + [pltpu.VMEM((8 * ACCS, 128), F32)] * ITEMS
        + ([] if before is None else later),
        cost_estimate=pl.CostEstimate(
            flops=2 * 10**9 * tiles, bytes_accessed=4 * 10**6 * tiles, transcendentals=0
        ),
        compiler_params=pltpu.CompilerParams(vmem_limit_bytes=40 << 20),
        name="sums",
    )(side, parts, *arrays)


def summed(parts_ref):
    total = parts_ref[0]
    for i in range(1, parts_ref.shape[0]):
        total = total + parts_ref[i]
    return total


def owned_kernel(parts_ref, out_ref):
    out_ref[...] = jnp.broadcast_to(summed(parts_ref)[None], out_ref.shape)


def finish_kernel(parts_ref, words_ref, levels_ref):
    total = summed(parts_ref)
    sums = total[:PIECE]
    group = (iota((128, 128), 0) >> 3 == iota((128, 128), 1) >> 3).astype(F32)
    squares = jnp.dot(sums * sums, group, precision=lax.Precision.HIGHEST, preferred_element_type=F32)
    words = sums / jnp.maximum(jnp.sqrt(squares), 1.0)
    words_ref[...] = jnp.broadcast_to(words[None], words_ref.shape)
    levels_ref[...] = total[PIECE : PIECE + 2] / jnp.maximum(total[PIECE + 2 : PIECE + 4], 1.0)


def simple(kernel, name, shapes, *arrays):
    out_shape = [jax.ShapeDtypeStruct(shape, F32) for shape in shapes]
    return pl.pallas_call(
        kernel,
        out_shape=out_shape,
        in_specs=vmem(len(arrays)),
        out_specs=vmem(len(shapes)),
        compiler_params=pltpu.CompilerParams(vmem_limit_bytes=16 << 20),
        name=name,
    )(*arrays)


def exchanged(array, axis):
    return lax.all_to_all(array, axis, 0, 0, tiled=True)


def per_device(weights, dir_codes, norm_bins):
    side = lax.axis_index("row")
    received = [
        exchanged(pack(chunk, weights, dir_codes.T, norm_bins.T), ("far", "near"))
        for chunk in range(len(CHUNKS))
    ]
    sums = None
    for chunk, parts in enumerate(received):
        sums = direction_sums(side.reshape(1), parts, chunk, sums)
    keep, send = sums
    joined = exchanged(keep + lax.ppermute(send, "row", [(0, 1), (1, 0)]), ("near", "cb"))
    (owned,) = simple(owned_kernel, "owned", [(FAR, PIECE + 8, 128)], joined)
    words, levels = simple(
        finish_kernel, "finish", [(2 * NEAR, PIECE, 128), (2, 128)], exchanged(owned, "far")
    )
    codewords = exchanged(words, ("near", "row"))
    return codewords.reshape(256, 128), levels.reshape(NBINS)


def solution(mesh):
    names = {"width": ("far", "near"), "cb": ("cb",), "row": ("row",)}
    sizes = {"far": FAR, "near": NEAR, "cb": mesh.shape["cb"], "row": mesh.shape["row"]}
    axes = tuple(part for name in mesh.axis_names for part in names[name])
    fine = jax.sharding.Mesh(mesh.devices.reshape([sizes[axis] for axis in axes]), axes)
    spec = P(("cb", "row"), ("far", "near"))
    return jax.shard_map(
        per_device,
        mesh=fine,
        in_specs=(spec,) * 3,
        out_specs=(P("cb", None), P()),
        check_vma=False,
    )
```

```python
import functools
import math

import jax
import jax.numpy as jnp
from jax import lax
from jax.experimental import pallas as pl
from jax.experimental.pallas import tpu as pltpu
from jax.sharding import PartitionSpec as P

WIDTH = 8192
CODES = 65536
NBINS = 256
SCALING = 1.0 / math.sqrt(WIDTH)
F32 = jnp.float32
I32 = jnp.int32

NEAR = 2
FAR = 8
PIECE = 128 // NEAR
SOURCES = NEAR * FAR
TILES = 14
CHUNKS = (10, 4)
BINNED = (6, 8)
LATE = CHUNKS[0] - BINNED[0]
ACCS = 8
ITEMS = 4
SCRATCH = 4 + 3 * ACCS + ITEMS
CODE_ROWS = CODES // 16


def iota(shape, axis):
    return lax.broadcasted_iota(I32, shape, axis)


def lanes_at(values, index):
    return jnp.take_along_axis(values, index, axis=1, mode="promise_in_bounds")


def vmem(count):
    return [pl.BlockSpec(memory_space=pltpu.VMEM)] * count


def chunk_rows(chunk):
    return -(-(9 * CHUNKS[chunk] + BINNED[chunk]) // 8) * 8


def place_in(counts, t):
    chunk = 0
    while t >= counts[chunk]:
        t -= counts[chunk]
        chunk += 1
    return chunk, t


def pack_kernel(wanted, weights_ref, codes_ref, bins_ref, out, lists_ref):
    common = jnp.bitwise_and(iota((128, 128), 0), iota((128, 128), 1))
    for shift in (4, 2, 1):
        common = jnp.bitwise_xor(common, common >> shift)
    hadamard = (1 - 2 * jnp.bitwise_and(common, 1)).astype(F32).astype(jnp.bfloat16)
    blocks = [
        jnp.dot(weights_ref[:, 128 * b : 128 * b + 128], hadamard, preferred_element_type=F32)
        for b in range(4)
    ]
    sums = [blocks[0] + blocks[1], blocks[0] - blocks[1], blocks[2] + blocks[3], blocks[2] - blocks[3]]
    blocks = [sums[0] + sums[2], sums[1] + sums[3], sums[0] - sums[2], sums[1] - sums[3]]
    lists_ref[:64, :448] = codes_ref[...].astype(F32)
    lists_ref[64:, :448] = bins_ref[...].astype(F32)
    lists = [lists_ref[:, 128 * i : 128 * i + 128].T for i in range(4)]
    lane = iota((8, 128), 1)
    own = jnp.bitwise_and(lane, 7) == iota((8, 128), 0)

    def spread(tile, column):
        block = lists[tile // 16][8 * (tile % 16) : 8 * (tile % 16) + 8, :]
        taken = lanes_at(block, column + (lane >> 3))
        return jnp.sum(jnp.where(own, taken, 0.0), axis=0, keepdims=True)

    for tile in range(56):
        for b in range(4):
            target, t = divmod(4 * tile + b, TILES)
            chunk, at = place_in(CHUNKS, t)
            tiles = CHUNKS[chunk]
            if chunk == wanted:
                out[target, 8 * at : 8 * at + 8, :] = blocks[b][8 * tile : 8 * tile + 8, :]
                out[target, 8 * tiles + at : 8 * tiles + at + 1, :] = spread(tile, 16 * b)
            chunk, at = place_in(BINNED, t)
            at += 9 * CHUNKS[chunk]
            if chunk == wanted:
                out[target, at : at + 1, :] = spread(tile, 64 + 16 * b)


def pack(wanted, weights, codes, bins):
    return pl.pallas_call(
        functools.partial(pack_kernel, wanted),
        out_shape=jax.ShapeDtypeStruct((SOURCES, chunk_rows(wanted), 128), F32),
        in_specs=vmem(3),
        out_specs=pl.BlockSpec(memory_space=pltpu.VMEM),
        cost_estimate=pl.CostEstimate(flops=10**9, bytes_accessed=2 * 10**6, transcendentals=0),
        scratch_shapes=[pltpu.VMEM((128, 512), F32)],
        name="pack",
    )(weights, codes, bins)


def sums_kernel(chunk, *refs):
    tiles, binned, first = CHUNKS[chunk], BINNED[chunk], chunk == 0
    inputs = 2 if first else 5
    outputs = 3 if first else 2
    side_ref, sent_ref = refs[:2]
    keep_ref, send_ref = refs[inputs : inputs + 2]
    scratch = refs[inputs + outputs :]
    at_sems, directions_ref, parts_ref, part_sem = scratch[:4]
    rows_refs, at_refs = scratch[4 : 4 + ACCS], scratch[4 + ACCS : 4 + 2 * ACCS]
    accs, items = scratch[4 + 2 * ACCS : 4 + 3 * ACCS], scratch[4 + 3 * ACCS : SCRATCH]
    arrival = pltpu.make_async_copy(sent_ref, parts_ref, part_sem)
    arrival.start()
    loads = []
    before = scratch[SCRATCH:]
    if not first:
        sums_sems, before = before[0], before[1:]
        loads = [pltpu.make_async_copy(refs[2 + i], before[i], sums_sems.at[i]) for i in range(2)]
        for load in loads:
            load.start()
    arrival.wait()
    lane = iota((8, 128), 1)
    place = iota((8, 128), 0)
    inner = jnp.bitwise_and(lane, 7)
    outer = lane >> 3
    for t in range(tiles):
        for h in range(SOURCES):
            row = parts_ref[h, 8 * tiles + t : 8 * tiles + t + 1, :].astype(I32) >> 4
            m = 2 * t + h // ACCS
            rows_refs[h % ACCS][m : m + 1, :] = row
    fetches = [
        pltpu.make_async_copy(rows_refs[j], at_refs[j], at_sems.at[j]) for j in range(ACCS)
    ]
    for fetch in fetches:
        fetch.start()
    share = -(-CODE_ROWS // (8 * tiles))
    group = (iota((128, 128), 0) >> 3 == iota((128, 128), 1) >> 3).astype(F32)

    def clear(t, offset):
        start = jnp.minimum(t * share, CODE_ROWS // 8 - share)
        for i in range(offset, share, 16):
            for acc in accs:
                acc[pl.ds(pl.multiple_of(8 * (start + i), 8), 8), :] = jnp.zeros((8, 128), F32)

    def bins_of(row):
        sums = []
        for half in range(2):
            bin_sum = jnp.zeros((8, 128), I32)
            for j in range(8):
                bins = parts_ref[8 * half + j, pl.ds(9 * tiles + row, 1), :]
                bins = lanes_at(jnp.broadcast_to(bins, (8, 128)).astype(I32), 8 * outer + place)
                bin_sum = bin_sum + jnp.where(inner == j, bins, 0)
            sums.append(bin_sum)
        return sums

    def counted(log_sums, bin_sums, carry):
        base = bin_sums[0] >> 4
        low, high, low_count, high_count = carry
        for offset in range(16):
            log_total = jnp.zeros((8, 128), F32)
            count = jnp.zeros((8, 128), F32)
            for log_sum, bin_sum in zip(log_sums, bin_sums):
                chosen = jnp.bitwise_and(bin_sum, 15) == offset
                log_total = log_total + jnp.where(chosen, log_sum, 0.0)
                count = count + jnp.where(chosen, 1.0, 0.0)
            log_total = jnp.sum(log_total, axis=1, keepdims=True)
            count = jnp.sum(count, axis=1, keepdims=True)
            target = 16 * base + offset
            at_low, at_high = target == lane, target == lane + 128
            low = low + jnp.where(at_low, log_total, 0.0)
            high = high + jnp.where(at_high, log_total, 0.0)
            low_count = low_count + jnp.where(at_low, count, 0.0)
            high_count = high_count + jnp.where(at_high, count, 0.0)
        return low, high, low_count, high_count

    def rotate(t):
        z = [parts_ref[h, pl.ds(pl.multiple_of(8 * t, 8), 8), :] for h in range(SOURCES)]
        for bit in range(4):
            d = 1 << bit
            z = [z[h ^ d] - z[h] if h & d else z[h] + z[h ^ d] for h in range(SOURCES)]
        rotated = jnp.concatenate(z, axis=0) * SCALING
        squares = jnp.dot(
            rotated * rotated, group, precision=lax.Precision.HIGHEST, preferred_element_type=F32
        )
        floored = jnp.maximum(jnp.sqrt(squares), 1.0)
        directions = rotated / floored
        logs = jnp.log(floored)
        for h in range(SOURCES):
            directions_ref[SOURCES * t + h] = directions[8 * h : 8 * h + 8]
        for offset in range(16):
            clear(t, offset)
        sums = []
        for half in range(2):
            log_sum = jnp.zeros((8, 128), F32)
            for j in range(8):
                h = 8 * half + j
                log_sum = log_sum + jnp.where(inner == j, logs[8 * h : 8 * h + 8], 0.0)
            sums.append(log_sum)
        return sums

    def rotate_and_count(t, carry):
        bin_sums = bins_of(t if first else t + LATE)
        return counted(rotate(t), bin_sums, carry)

    empty = jnp.zeros((8, 128), F32)
    bin_parts = (empty,) * 4
    if first:
        for t in range(binned, tiles):
            for half, log_sum in enumerate(rotate(t)):
                refs[inputs + 2][2 * (t - binned) + half] = log_sum
    else:
        for row in range(LATE):
            late = [refs[4][2 * row + half] for half in range(2)]
            bin_parts = counted(late, bins_of(row), bin_parts)
    bin_parts = lax.fori_loop(0, min(tiles, binned), rotate_and_count, bin_parts)
    rows = [jnp.sum(part, axis=0, keepdims=True) for part in bin_parts]
    totals = jnp.concatenate(rows + [jnp.zeros((4, 128), F32)], axis=0)

    for fetch in fetches:
        fetch.wait()

    def step(m, carry):
        t, half = m >> 1, jnp.bitwise_and(m, 1)
        moved = [directions_ref[ACCS * m + j] for j in range(ACCS)]
        slots = []
        for j in range(ACCS):
            row = parts_ref[ACCS * half + j, pl.ds(8 * tiles + t, 1), :]
            slots.append(jnp.bitwise_and(jnp.broadcast_to(row, (8, 128)).astype(I32), 15))
        for k in range(16):
            items_ref = items[k % len(items)]
            for j in range(ACCS):
                values = lanes_at(moved[j], 8 * k + inner)
                slot = lanes_at(slots[j], 8 * k + place)
                items_ref[8 * j : 8 * j + 8, :] = jnp.where(slot == outer, values, 0.0)
            for s in range(8):
                at = [at_refs[j][m, 8 * k + s] for j in range(ACCS)]
                old = [accs[j][pl.ds(at[j], 1), :] for j in range(ACCS)]
                for j in range(ACCS):
                    accs[j][pl.ds(at[j], 1), :] = old[j] + items_ref[8 * j + s : 8 * j + s + 1, :]
        return carry

    lax.fori_loop(0, 2 * tiles, step, 0)
    side = side_ref[0]

    owners = CODE_ROWS // 256
    for load in loads:
        load.wait()

    def finish(c, carry):
        for i, ref, mine in ((0, keep_ref, side), (1, send_ref, 1 - side)):
            for near in range(NEAR):
                start = pl.multiple_of(c * 256 + (2 * near + mine) * PIECE, PIECE)
                total = accs[0][pl.ds(start, PIECE), :]
                for acc in accs[1:]:
                    total = total + acc[pl.ds(start, PIECE), :]
                to = near * owners + c
                ref[to, :PIECE] = total if first else total + before[i][to, :PIECE]
                ref[to, PIECE:] = totals if first else totals + before[i][to, PIECE:]
        return carry

    lax.fori_loop(0, owners, finish, 0)


def direction_sums(side, parts, chunk, before):
    tiles, shape = CHUNKS[chunk], (NEAR * CODE_ROWS // 256, PIECE + 8, 128)
    arrays = () if before is None else tuple(before)
    later = [pltpu.SemaphoreType.DMA((2,))] + [pltpu.VMEM(shape, F32)] * 2
    anywhere = pl.BlockSpec(memory_space=pl.ANY)
    logs = [jax.ShapeDtypeStruct((2 * LATE, 8, 128), F32)]
    return pl.pallas_call(
        functools.partial(sums_kernel, chunk),
        out_shape=[jax.ShapeDtypeStruct(shape, F32)] * 2 + (logs if before is None else []),
        in_specs=[pl.BlockSpec(memory_space=pltpu.SMEM), anywhere]
        + ([] if before is None else [anywhere] * 2 + vmem(1)),
        out_specs=vmem(3 if before is None else 2),
        scratch_shapes=[
            pltpu.SemaphoreType.DMA((ACCS,)),
            pltpu.VMEM((SOURCES * tiles, 8, 128), F32),
            pltpu.VMEM(parts.shape, F32),
            pltpu.SemaphoreType.DMA,
        ]
        + [pltpu.VMEM((2 * tiles, 128), I32)] * ACCS
        + [pltpu.SMEM((2 * tiles, 128), I32)] * ACCS
        + [pltpu.VMEM((CODE_ROWS, 128), F32)] * ACCS
        + [pltpu.VMEM((8 * ACCS, 128), F32)] * ITEMS
        + ([] if before is None else later),
        cost_estimate=pl.CostEstimate(
            flops=2 * 10**9 * tiles, bytes_accessed=4 * 10**6 * tiles, transcendentals=0
        ),
        compiler_params=pltpu.CompilerParams(vmem_limit_bytes=40 << 20),
        name="sums",
    )(side, parts, *arrays)


def summed(parts_ref):
    total = parts_ref[0]
    for i in range(1, parts_ref.shape[0]):
        total = total + parts_ref[i]
    return total


def owned_kernel(parts_ref, out_ref):
    out_ref[...] = jnp.broadcast_to(summed(parts_ref)[None], out_ref.shape)


def finish_kernel(parts_ref, words_ref, levels_ref):
    total = summed(parts_ref)
    sums = total[:PIECE]
    group = (iota((128, 128), 0) >> 3 == iota((128, 128), 1) >> 3).astype(F32)
    squares = jnp.dot(sums * sums, group, precision=lax.Precision.HIGHEST, preferred_element_type=F32)
    words = sums / jnp.maximum(jnp.sqrt(squares), 1.0)
    words_ref[...] = jnp.broadcast_to(words[None], words_ref.shape)
    levels_ref[...] = total[PIECE : PIECE + 2] / jnp.maximum(total[PIECE + 2 : PIECE + 4], 1.0)


def simple(kernel, name, shapes, *arrays):
    out_shape = [jax.ShapeDtypeStruct(shape, F32) for shape in shapes]
    return pl.pallas_call(
        kernel,
        out_shape=out_shape,
        in_specs=vmem(len(arrays)),
        out_specs=vmem(len(shapes)),
        compiler_params=pltpu.CompilerParams(vmem_limit_bytes=16 << 20),
        name=name,
    )(*arrays)


def exchanged(array, axis):
    return lax.all_to_all(array, axis, 0, 0, tiled=True)


def per_device(weights, dir_codes, norm_bins):
    side = lax.axis_index("row")
    received = [
        exchanged(pack(chunk, weights, dir_codes.T, norm_bins.T), ("far", "near"))
        for chunk in range(len(CHUNKS))
    ]
    sums = None
    for chunk, parts in enumerate(received):
        sums = direction_sums(side.reshape(1), parts, chunk, sums)
    keep, send = sums
    joined = exchanged(keep + lax.ppermute(send, "row", [(0, 1), (1, 0)]), ("near", "cb"))
    (owned,) = simple(owned_kernel, "owned", [(FAR, PIECE + 8, 128)], joined)
    words, levels = simple(
        finish_kernel, "finish", [(2 * NEAR, PIECE, 128), (2, 128)], exchanged(owned, "far")
    )
    codewords = exchanged(words, ("near", "row"))
    return codewords.reshape(256, 128), levels.reshape(NBINS)


def solution(mesh):
    names = {"width": ("far", "near"), "cb": ("cb",), "row": ("row",)}
    sizes = {"far": FAR, "near": NEAR, "cb": mesh.shape["cb"], "row": mesh.shape["row"]}
    axes = tuple(part for name in mesh.axis_names for part in names[name])
    fine = jax.sharding.Mesh(mesh.devices.reshape([sizes[axis] for axis in axes]), axes)
    spec = P(("cb", "row"), ("far", "near"))
    return jax.shard_map(
        per_device,
        mesh=fine,
        in_specs=(spec,) * 3,
        out_specs=(P("cb", None), P()),
        check_vma=False,
    )
```
